32 devices in a mesh: dp: 4 (over y, x), tensor: 8 (over z, core).
Axes of the slice: x: 2, y: 2, z: 4, core: 2. Of those that a mesh axis runs over, the one named last changes fastest.
Arguments:
- tokens: bfloat16 [8192, 2048], P(('dp', 'tensor')), may hold values from -6 to 6
- cotangent: bfloat16 [8192, 2048], P(('dp', 'tensor')), may hold values from -6 to 6
- ln_gain: float32 [2048], replicated, may hold values from 0.5 to 1.5
- ln_shift: float32 [2048], replicated, may hold values from -3 to 3
- w_qkv: bfloat16 [2048, 3, 2048], P(None, None, 'tensor'), may hold values from -0.125 to 0.125
- b_qkv: float32 [3, 2048], P(None, 'tensor'), may hold values from -3 to 3
- w_out: bfloat16 [2048, 2048], P('tensor'), may hold values from -0.5 to 0.5
- w_up: bfloat16 [2048, 8192], P(None, 'tensor'), may hold values from -0.125 to 0.125
- b_up: float32 [8192], P('tensor'), may hold values from -3 to 3
- w_down: bfloat16 [8192, 2048], P('tensor'), may hold values from -0.0625 to 0.0625
- out_bias: float32 [2048], replicated, may hold values from -3 to 3
Outputs:
- result: bfloat16 [8192, 2048], P(('dp', 'tensor'))
- token_grad: float32 [8192, 2048], P(('dp', 'tensor'))
- ln_gain_grad: float32 [2048], replicated
- ln_shift_grad: float32 [2048], replicated
- w_qkv_grad: float32 [2048, 3, 2048], P(None, None, 'tensor')
- b_qkv_grad: float32 [3, 2048], P(None, 'tensor')
- w_out_grad: float32 [2048, 2048], P('tensor')
- w_up_grad: float32 [2048, 8192], P(None, 'tensor')
- b_up_grad: float32 [8192], P('tensor')
- w_down_grad: float32 [8192, 2048], P('tensor')
- out_bias_grad: float32 [2048], replicated
The draws below stay inside these ranges and needn't reach their ends.
All inputs are finite; a program needn't handle non-finite values.
Results may differ from the reference program's by a relative error of at most 0.012.
The reference program's roundings to bfloat16 on the way count: a program that leaves them out, or rounds other values in their place, can miss the bound.
Values may be sent and summed in bfloat16 or wider, within the bound.
No kernel may reach another device: no remote copies, remote signals or barrier semaphores. Data moves between devices by JAX's collectives and lax.ppermute only.
A program may use at most 192 MiB of HBM per device.

```python
import jax
import jax.numpy as jnp
from jax import lax

D = 2048
HEADS = 32
HEAD_DIM = 64
ROT = 32
FF = 8192
LENGTH = 2048
SEQS = 1
TOKENS = 8192
N_DP = 4


def level_of(rng, dims, cuts, smallest, high):
    gain, own = 1.0, jax.random.fold_in(rng, 6)
    for position, shards_of in cuts:
        steps = jnp.exp(jax.random.uniform(jax.random.fold_in(own, position), (shards_of,), jnp.float32, smallest / len(cuts), high / len(cuts)))
        gain = gain * jnp.repeat(steps, dims[position] // shards_of).reshape([-1 if axis == position else 1 for axis in range(len(dims))])
    return gain


def normal_values(own_key, extent, width, limit, shards=(), held_as=jnp.bfloat16):
    level = level_of(own_key, extent, shards, -0.22, 0.18) if shards else 1.0
    values = jax.random.normal(own_key, extent, jnp.float32) * width * level
    return jnp.minimum(jnp.maximum(values, -limit), limit).astype(held_as)


def setup_inputs(seed: int = 0) -> dict:
    arg_keys = jax.random.split(jax.random.key(seed), 12)
    tokens = normal_values(arg_keys[0], (TOKENS, D), 1.0, 6.0, ((0, 32),))
    cotangent = normal_values(arg_keys[1], (TOKENS, D), 1.0, 6.0, ((0, 32),))
    ln_gain = jnp.clip(1.0 + 0.1 * jax.random.normal(arg_keys[2], (D,), jnp.float32), 0.5, 1.5)
    ln_shift = normal_values(arg_keys[3], (D,), 0.5, 3.0, (), jnp.float32)
    w_qkv = normal_values(arg_keys[4], (D, 3, HEADS * HEAD_DIM), D ** -0.5, 0.125, ((2, 8),))
    b_qkv = normal_values(arg_keys[5], (3, HEADS * HEAD_DIM), 0.5, 3.0, ((1, 8),), jnp.float32)
    w_out = normal_values(arg_keys[6], (HEADS * HEAD_DIM, D), (HEADS * HEAD_DIM // 16) ** -0.5, 0.5, ((0, 8),))
    w_up = normal_values(arg_keys[7], (D, FF), D ** -0.5, 0.125, ((1, 8),))
    b_up = normal_values(arg_keys[8], (FF,), 0.5, 3.0, ((0, 8),), jnp.float32)
    w_down = normal_values(arg_keys[9], (FF, D), FF ** -0.5, 0.0625, ((0, 8),))
    out_bias = normal_values(arg_keys[10], (D,), 0.5, 3.0, (), jnp.float32)
    return dict(tokens=tokens, cotangent=cotangent, ln_gain=ln_gain, ln_shift=ln_shift, w_qkv=w_qkv, b_qkv=b_qkv, w_out=w_out, w_up=w_up, b_up=b_up, w_down=w_down, out_bias=out_bias)


EPSILON = 1e-05
ROTARY_BASE = 10000.0
HIGHEST = lax.Precision.HIGHEST

@jax.custom_vjp
def low(v):
    return lax.optimization_barrier(v.astype(jnp.bfloat16)).astype(jnp.float32)

@jax.custom_vjp
def low_back(v):
    return v

def low_keep(v):
    return (low(v), None)

def low_pass(kept, grad):
    return (grad,)

def back_keep(v):
    return (v, None)

def back_low(kept, grad):
    return (low(grad),)
low.defvjp(low_keep, low_pass)
low_back.defvjp(back_keep, back_low)

def layer_norm(row_data, norm_gain, norm_shift):
    average = lax.optimization_barrier(jnp.mean(row_data, axis=-1, keepdims=True))
    centred = row_data - average
    variance = lax.optimization_barrier(jnp.mean(centred * centred, axis=-1, keepdims=True))
    return centred * lax.rsqrt(variance + EPSILON) * norm_gain + norm_shift

def rotate(head_data, positions, rot_dims):
    half_dims = rot_dims // 2
    frequency = ROTARY_BASE ** (-2.0 * jnp.arange(half_dims).astype(jnp.float32) / rot_dims)
    angles = positions.astype(jnp.float32)[:, None] * frequency[None, :]
    cosine = jnp.cos(angles)[:, None, :]
    sine = jnp.sin(angles)[:, None, :]
    first_half = head_data[..., :half_dims]
    second_half = head_data[..., half_dims:rot_dims]
    return jnp.concatenate([first_half * cosine - second_half * sine, second_half * cosine + first_half * sine, head_data[..., rot_dims:]], axis=-1)

def attend_head(pieces):
    queries, keys_low, values = pieces
    scores = low_back(jnp.einsum('sqd,skd->sqk', queries, keys_low, precision=HIGHEST) * HEAD_DIM ** (-0.5))
    causal = jnp.arange(LENGTH)[:, None] >= jnp.arange(LENGTH)[None, :]
    scores = jnp.where(causal[None], scores, -1e+30)
    weights = low(jax.nn.softmax(scores, axis=-1))
    return jnp.einsum('sqk,skd->sqd', weights, values, precision=HIGHEST)

def to_heads(head_rows):
    return jnp.transpose(head_rows.reshape(SEQS, LENGTH, HEADS, HEAD_DIM), (2, 0, 1, 3))

def forward_group(rows_in, norm_gain, norm_shift, qkv_weight, qkv_bias, out_weight, up_weight, up_bias, down_weight, shared_bias):
    row_total = rows_in.shape[0]
    normed = low(layer_norm(rows_in, norm_gain, norm_shift))
    projected = low_back(jnp.dot(normed, qkv_weight.reshape(D, 3 * HEADS * HEAD_DIM), precision=HIGHEST) + qkv_bias.reshape(1, 3 * HEADS * HEAD_DIM))
    projected = projected.reshape(row_total, 3, HEADS, HEAD_DIM)
    positions = jnp.arange(row_total) % LENGTH
    queries = low(rotate(projected[:, 0], positions, ROT))
    keys_low = low(rotate(projected[:, 1], positions, ROT))
    values = low(projected[:, 2])
    mixed_heads = lax.map(jax.checkpoint(attend_head), (to_heads(queries), to_heads(keys_low), to_heads(values)))
    mixed = jnp.transpose(mixed_heads, (1, 2, 0, 3)).reshape(row_total, HEADS * HEAD_DIM)
    mixed = low_back(low(mixed))
    attention_out = low_back(jnp.dot(mixed, out_weight, precision=HIGHEST))
    pre_act = low_back(jnp.dot(normed, up_weight, precision=HIGHEST) + up_bias)
    hidden = low(jax.nn.gelu(pre_act, approximate=True))
    feedforward_out = low_back(jnp.dot(hidden, down_weight, precision=HIGHEST))
    return rows_in + attention_out + feedforward_out + shared_bias

def reference(tokens, cotangent, ln_gain, ln_shift, w_qkv, b_qkv, w_out, w_up, b_up, w_down, out_bias):
    params = tuple((entry.astype(jnp.float32) for entry in (ln_gain, ln_shift, w_qkv, b_qkv, w_out, w_up, b_up, w_down, out_bias)))
    group_rows = SEQS * LENGTH
    inputs = tokens.astype(jnp.float32).reshape(N_DP, group_rows, D)
    pull_rows = cotangent.astype(jnp.float32).reshape(N_DP, group_rows, D)
    zeros = tuple((jnp.zeros_like(entry) for entry in params))

    def one_group(totals, group_pair):
        rows_in, grad_in = group_pair
        output, pullback = jax.vjp(forward_group, rows_in, *params)
        gradients = pullback(grad_in)
        totals = tuple((total + extra for total, extra in zip(totals, gradients[1:])))
        return (totals, (output.astype(jnp.bfloat16), gradients[0]))
    totals, (outputs, input_grads) = lax.scan(one_group, zeros, (inputs, pull_rows))
    return (outputs.reshape(TOKENS, D), input_grads.reshape(TOKENS, D), totals[0], totals[1], totals[2], totals[3], totals[4], totals[5], totals[6], totals[7], totals[8])
```

```python
from functools import partial
import jax, jax.numpy as jnp
from jax import lax
from jax.experimental import pallas as pl
from jax.experimental.pallas import tpu as pltpu
from jax.sharding import PartitionSpec as P

HEAD_DIM = 64
ROT = 32
LENGTH = 2048
EPSILON = 1e-05
ROTARY_BASE = 10000.0
LOG2E = 1.4426950408889634
F32 = jnp.float32
BF16 = jnp.bfloat16
NEG = -1e30


def mm(a, b, ca, cb):
    return lax.dot_general(a, b, (((ca,), (cb,)), ((), ())), preferred_element_type=F32)


def turn(u, cos, sin):
    h = ROT // 2
    a, b = u[:h], u[h:ROT]
    return jnp.concatenate([a * cos - b * sin, b * cos + a * sin, u[ROT:]], axis=0)


def attend_kernel(block, proj_ref, bias_ref, cos_ref, sin_ref, qt_ref, kt_ref, vt_ref, o_ref, lse_ref, k_ref):
    length = proj_ref.shape[-1]
    cos, sin = cos_ref[...], sin_ref[...]
    qt_ref[0] = turn(proj_ref[0, 0] + bias_ref[0, 0], cos, sin).astype(BF16)
    kt = turn(proj_ref[1, 0] + bias_ref[1, 0], cos, sin)
    kt_ref[0] = kt.astype(BF16)
    k_ref[...] = kt.T.astype(BF16)
    vt_ref[0] = (proj_ref[2, 0] + bias_ref[2, 0]).astype(BF16)
    scale = HEAD_DIM ** (-0.5) * LOG2E
    rows = lax.broadcasted_iota(jnp.int32, (block, block), 0)
    cols = lax.broadcasted_iota(jnp.int32, (block, block), 1)

    def step(qt, carry, ki, masked):
        top, total, acc = carry
        ks = pl.ds(pl.multiple_of(ki * block, block), block)
        s = mm(k_ref[ks, :], qt, 1, 0) * scale
        if masked:
            s = jnp.where(rows <= cols, s, NEG)
        new = jnp.maximum(top, jnp.max(s, axis=0, keepdims=True))
        p = jnp.exp2(s - new)
        fade = jnp.exp2(top - new)
        total = total * fade + jnp.sum(p, axis=0, keepdims=True)
        acc = acc * fade + mm(vt_ref[0, :, ks], p.astype(BF16), 1, 0)
        return new, total, acc

    def one(qi, _):
        qs = pl.ds(pl.multiple_of(qi * block, block), block)
        qt = qt_ref[0, :, qs]
        carry = (
            jnp.full((1, block), NEG, F32),
            jnp.zeros((1, block), F32),
            jnp.zeros((HEAD_DIM, block), F32),
        )
        carry = step(qt, carry, qi, True)
        top, total, acc = lax.fori_loop(0, qi, lambda ki, c: step(qt, c, ki, False), carry)
        o_ref[0, :, qs] = acc / total
        lse_ref[0, :, qs] = top + jnp.log2(total)
        return 0

    lax.fori_loop(0, length // block, one, 0)


def attend(proj, bias, cos, sin, block=512):
    _, heads, _, length = proj.shape
    head = pl.BlockSpec((1, HEAD_DIM, length), lambda h: (h, 0, 0))
    return pl.pallas_call(
        partial(attend_kernel, block),
        grid=(heads,),
        in_specs=[
            pl.BlockSpec((3, 1, HEAD_DIM, length), lambda h: (0, h, 0, 0)),
            pl.BlockSpec((3, 1, HEAD_DIM, 1), lambda h: (0, h, 0, 0)),
            pl.BlockSpec((ROT // 2, length), lambda h: (0, 0)),
            pl.BlockSpec((ROT // 2, length), lambda h: (0, 0)),
        ],
        out_specs=[head, head, head, head, pl.BlockSpec((1, 1, length), lambda h: (h, 0, 0))],
        out_shape=[
            jax.ShapeDtypeStruct((heads, HEAD_DIM, length), BF16),
            jax.ShapeDtypeStruct((heads, HEAD_DIM, length), BF16),
            jax.ShapeDtypeStruct((heads, HEAD_DIM, length), BF16),
            jax.ShapeDtypeStruct((heads, HEAD_DIM, length), F32),
            jax.ShapeDtypeStruct((heads, 1, length), F32),
        ],
        scratch_shapes=[pltpu.VMEM((length, HEAD_DIM), BF16)],
        compiler_params=pltpu.CompilerParams(vmem_limit_bytes=40 << 20),
        cost_estimate=pl.CostEstimate(flops=heads * length * length * 512, bytes_accessed=heads * length * 64 * 22, transcendentals=0),
        name="attend",
    )(proj, bias, cos, sin)


def retreat_kernel(block, qt_ref, kt_ref, vt_ref, o_ref, lse_ref, dot_ref, cos_ref, sin_ref, out_ref,
                   q_ref, k_ref, v_ref, do_ref, delta_ref, dqt_ref, dk_ref, dv_ref):
    length = qt_ref.shape[-1]
    n = length // block
    q_ref[...] = qt_ref[0].astype(F32).T.astype(BF16)
    k_ref[...] = kt_ref[0].astype(F32).T.astype(BF16)
    v_ref[...] = vt_ref[0].astype(F32).T.astype(BF16)
    dot32 = dot_ref[0].astype(F32)
    do_ref[...] = dot32.T.astype(BF16)
    delta_ref[...] = jnp.sum(dot32 * o_ref[0], axis=0, keepdims=True)
    scale = HEAD_DIM ** (-0.5) * LOG2E
    rows = lax.broadcasted_iota(jnp.int32, (block, block), 0)
    cols = lax.broadcasted_iota(jnp.int32, (block, block), 1)

    def step(ki, qi, masked):
        ks = pl.ds(pl.multiple_of(ki * block, block), block)
        qs = pl.ds(pl.multiple_of(qi * block, block), block)
        s = mm(k_ref[ks, :], qt_ref[0, :, qs], 1, 0) * scale - lse_ref[0, :, qs]
        if masked:
            s = jnp.where(rows <= cols, s, NEG)
        p = jnp.exp2(s)
        dp = mm(v_ref[ks, :], dot_ref[0, :, qs], 1, 0)
        ds = (p * (dp - delta_ref[:, qs])).astype(BF16)
        dv = mm(p.astype(BF16), do_ref[qs, :], 1, 0)
        dk = mm(ds, q_ref[qs, :], 1, 0)
        dq = mm(kt_ref[0, :, ks], ds, 1, 0)
        return qs, dq, dk, dv

    def one(ki, _):
        ks = pl.ds(pl.multiple_of(ki * block, block), block)
        qs, dq, dk, dv = step(ki, ki, True)

        @pl.when(ki == 0)
        def _():
            dqt_ref[:, qs] = dq

        @pl.when(ki > 0)
        def _():
            dqt_ref[:, qs] += dq

        dk_ref[ks, :] = dk
        dv_ref[ks, :] = dv

        def more(qi, c):
            qs, dq, dk, dv = step(ki, qi, False)

            @pl.when(ki == 0)
            def _():
                dqt_ref[:, qs] = dq

            @pl.when(ki > 0)
            def _():
                dqt_ref[:, qs] += dq

            dk_ref[ks, :] += dk
            dv_ref[ks, :] += dv
            return c

        lax.fori_loop(ki + 1, n, more, 0)
        return 0

    lax.fori_loop(0, n, one, 0)
    cos, sin = cos_ref[...], -sin_ref[...]
    back = HEAD_DIM ** (-0.5)
    out_ref[0, 0] = turn(dqt_ref[...] * back, cos, sin).astype(BF16)
    out_ref[1, 0] = turn(dk_ref[...].T * back, cos, sin).astype(BF16)
    out_ref[2, 0] = dv_ref[...].T.astype(BF16)


def retreat(qt, kt, vt, o, lse, dot, cos, sin, block=512):
    heads, _, length = qt.shape
    head = pl.BlockSpec((1, HEAD_DIM, length), lambda h: (h, 0, 0))
    table = pl.BlockSpec((ROT // 2, length), lambda h: (0, 0))
    return pl.pallas_call(
        partial(retreat_kernel, block),
        grid=(heads,),
        in_specs=[head, head, head, head, pl.BlockSpec((1, 1, length), lambda h: (h, 0, 0)), head, table, table],
        out_specs=pl.BlockSpec((3, 1, HEAD_DIM, length), lambda h: (0, h, 0, 0)),
        out_shape=jax.ShapeDtypeStruct((3, heads, HEAD_DIM, length), BF16),
        scratch_shapes=[pltpu.VMEM((length, HEAD_DIM), BF16)] * 4
        + [pltpu.VMEM((1, length), F32), pltpu.VMEM((HEAD_DIM, length), F32)]
        + [pltpu.VMEM((length, HEAD_DIM), F32)] * 2,
        compiler_params=pltpu.CompilerParams(vmem_limit_bytes=40 << 20),
        cost_estimate=pl.CostEstimate(flops=heads * length * length * 1280, bytes_accessed=heads * length * 64 * 20, transcendentals=0),
        name="retreat",
    )(qt, kt, vt, o, lse, dot, cos, sin)


def tables(length):
    half = ROT // 2
    frequency = ROTARY_BASE ** (-2.0 * jnp.arange(half).astype(F32) / ROT)
    angles = frequency[:, None] * jnp.arange(length).astype(F32)[None, :]
    return jnp.cos(angles), jnp.sin(angles)


class Box:
    def __init__(self, value):
        self.value = value


class Line:
    def __init__(self):
        self.last = []

    def run(self, stage, *boxes):
        held = list(dict.fromkeys(list(boxes) + self.last))
        for box, value in zip(held, lax.optimization_barrier(tuple(box.value for box in held))):
            box.value = value
        made = [Box(value) for value in stage(*[box.value for box in boxes])]
        self.last = made
        return made


def rows_of(value, start, size):
    return lax.dynamic_slice_in_dim(value, start, size, 0)


def ordered(bit, mine, other):
    return [jnp.where(bit == 0, mine, other), jnp.where(bit == 0, other, mine)]


class Exchange:
    def __init__(self, line, grad, axis):
        self.line, self.grad, self.axis = line, grad, axis
        me = lax.axis_index(axis)
        self.low, self.high = me % 2, me // 2
        self.phase = 0

    def swap(self, box, bit):
        return Box(lax.ppermute(box.value, self.axis, [(i, i ^ bit) for i in range(4)]))

    def send(self):
        quarter = self.grad.value.shape[0] // 4

        def stage(grad):
            return (
                rows_of(grad, (1 - self.low) * quarter, quarter),
                rows_of(grad, (3 - self.high) * quarter, quarter),
            )

        a, b = self.line.run(stage, self.grad)
        self.got = self.swap(a, 1), self.swap(b, 2)

    def fold(self):
        quarter = self.grad.value.shape[0] // 4
        eighth = quarter // 2
        low, high = self.low, self.high

        def stage(grad, a, b):
            def part(got, start, bit):
                return rows_of(grad, start + bit * eighth, eighth).astype(F32) + rows_of(got, bit * eighth, eighth).astype(F32)

            at_a, at_b = low * quarter, (2 + high) * quarter
            return (
                part(a, at_a, 1 - high).astype(BF16),
                part(b, at_b, 1 - low).astype(BF16),
                part(a, at_a, high),
                part(b, at_b, low),
            )

        a, b, self.keep_a, self.keep_b = self.line.run(stage, self.grad, *self.got)
        self.got = self.swap(a, 2), self.swap(b, 1)

    def close(self):
        def stage(keep_a, keep_b, a, b):
            return (keep_a + a.astype(F32)).astype(BF16), (keep_b + b.astype(F32)).astype(BF16)

        self.sums = self.line.run(stage, self.keep_a, self.keep_b, *self.got)
        self.got = self.swap(self.sums[0], 2), self.swap(self.sums[1], 1)

    def share(self):
        def stage(mine_a, mine_b, a, b):
            return (
                jnp.concatenate(ordered(self.high, mine_a, a), axis=0),
                jnp.concatenate(ordered(self.low, mine_b, b), axis=0),
            )

        self.sums = self.line.run(stage, *self.sums, *self.got)
        self.got = self.swap(self.sums[0], 1), self.swap(self.sums[1], 2)

    def parts(self):
        return [*self.sums, *self.got]

    def whole(self, mine_a, mine_b, a, b):
        return jnp.concatenate(ordered(self.low, mine_a, a) + ordered(self.high, mine_b, b), axis=0).astype(F32)

    def step(self):
        self.phase += 1
        (self.send, self.fold, self.close, self.share)[self.phase - 1]()


class Plain:
    def __init__(self, line, grad, axis):
        self.grad, self.axis = grad, axis

    def step(self):
        if self.grad is not None:
            self.sum = Box(lax.psum(self.grad.value, self.axis))
            self.grad = None

    def parts(self):
        return [self.sum]

    def whole(self, total):
        return total.astype(F32)


def small_sum(value, axis):
    count = lax.axis_size(axis)
    bit = 1
    while bit < count:
        value = value + lax.ppermute(value, axis, [(i, i ^ bit) for i in range(count)])
        bit *= 2
    return value


def per_device(
    tokens, cotangent, ln_gain, ln_shift, w_qkv, b_qkv, w_out, w_up, b_up, w_down, out_bias
):
    axis = "tensor"
    share, width = tokens.shape
    rows = share * lax.axis_size(axis)
    head_cols = w_qkv.shape[2]
    heads = head_cols // HEAD_DIM
    units = b_up.shape[0]
    half = width // 2
    exchange = Exchange if lax.axis_size("dp") == 4 else Plain
    line = Line()
    run = line.run

    own = tokens.astype(F32)
    average = jnp.mean(own, axis=-1, keepdims=True)
    centred = own - average
    rsig = lax.rsqrt(jnp.mean(centred * centred, axis=-1, keepdims=True) + EPSILON)
    xhat = centred * rsig

    def gather(box):
        return Box(lax.all_gather(box.value, axis, axis=0, tiled=True))

    normed = gather(Box((xhat * ln_gain + ln_shift).astype(BF16)))
    cot = Box(cotangent)
    left, right = run(lambda n, c: (c[:, :half], c[:, half:]), normed, cot)
    pull0 = gather(left)
    w3 = jnp.transpose(w_qkv, (1, 0, 2))
    cos, sin = tables(LENGTH)

    def rise(n):
        pre = jnp.dot(n, w_up, preferred_element_type=F32) + b_up
        return jax.nn.gelu(pre, approximate=True).astype(BF16), pre

    hidden, pre = run(rise, normed)

    def project(n):
        return (lax.dot_general(w3, n, (((1,), (1,)), ((), ())), preferred_element_type=F32),)

    (proj,) = run(project, normed)
    seqs = rows // LENGTH

    def look(p):
        p = p.reshape(3, heads, HEAD_DIM, seqs, LENGTH).transpose(0, 3, 1, 2, 4).reshape(3, seqs * heads, HEAD_DIM, LENGTH)
        bias = jnp.tile(b_qkv.reshape(3, heads, HEAD_DIM, 1), (1, seqs, 1, 1))
        qt, kt, vt, o32, lse = attend(p, bias, cos, sin, 1024)
        mixed = o32.astype(BF16).reshape(seqs, head_cols, LENGTH).transpose(1, 0, 2).reshape(head_cols, rows)
        return mixed, qt, kt, vt, o32, lse

    mixed, qt, kt, vt, o32, lse = run(look, proj)

    def down_grad(h, c):
        return (mm(h, c, 0, 0).astype(BF16),)

    (grad0,) = run(down_grad, hidden, pull0)
    pull0.value, right.value = lax.optimization_barrier((pull0.value, right.value))
    pull1 = gather(right)
    down0 = exchange(line, grad0, "dp")
    down0.step()

    def spread(m, h):
        return ((mm(m, w_out, 0, 0) + mm(h, w_down, 1, 0)).astype(BF16),)

    (branch,) = run(spread, mixed, hidden)
    branch = Box(lax.psum_scatter(branch.value, axis, scatter_dimension=0, tiled=True))
    down0.step()

    def first_pull(c, m):
        return mm(c, w_down[:, :half], 1, 1), mm(w_out[:, :half], c, 1, 1), mm(m, c, 1, 0).astype(BF16)

    d_hidden0, d_mixed0, out0 = run(first_pull, pull0, mixed)
    down0.step()
    (grad1,) = run(down_grad, hidden, pull1)
    down0.step()
    down1 = exchange(line, grad1, "dp")
    down1.step()

    def second_pull(c, d, m, o):
        return (d + mm(w_out[:, half:], c, 1, 1)).astype(BF16), jnp.concatenate([o, mm(m, c, 1, 0).astype(BF16)], axis=1)

    d_mixed, out_grad = run(second_pull, pull1, d_mixed0, mixed, out0)

    def d_rise(c, d, p):
        d = d + mm(c, w_down[:, half:], 1, 1)
        d = jax.vjp(partial(jax.nn.gelu, approximate=True), p)[1](d)[0].astype(BF16)
        return d, jnp.sum(d, axis=0, dtype=F32)

    d_pre, b_up_part = run(d_rise, pull1, d_hidden0, pre)
    down1.step()
    out = exchange(line, out_grad, "dp")
    out.step()

    def up_grad(n, d):
        return (mm(n, d, 0, 0).astype(BF16),)

    top = Box(None)
    (grad2,) = run(lambda n, d: up_grad(n[:, :half], d), normed, d_pre)
    down1.step()
    up0 = exchange(line, grad2, "dp")
    up0.step()
    out.step()

    def relook(d, qt, kt, vt, o32, lse):
        d = d.reshape(heads, HEAD_DIM, seqs, LENGTH).transpose(2, 0, 1, 3).reshape(seqs * heads, HEAD_DIM, LENGTH)
        d = retreat(qt, kt, vt, o32, lse, d, cos, sin, 512)
        return (d.reshape(3, seqs, head_cols, LENGTH).transpose(0, 2, 1, 3).reshape(3 * head_cols, rows),)

    (d_qkv,) = run(relook, d_mixed, qt, kt, vt, o32, lse)
    out.step()
    down1.step()
    up0.step()
    out.step()
    w_flat = w3.transpose(0, 2, 1).reshape(3 * head_cols, width)

    def back(d, p):
        return ((mm(d, w_flat, 0, 0) + mm(p, w_up, 1, 1)).astype(BF16),)

    (d_normed,) = run(back, d_qkv, d_pre)
    d_normed = Box(lax.psum_scatter(d_normed.value, axis, scatter_dimension=0, tiled=True))
    up0.step()
    (grad3,) = run(lambda n, d: up_grad(n[:, half:], d), normed, d_pre)
    up1 = exchange(line, grad3, "dp")
    up1.step()
    up0.step()

    def qkv_grad(d, n):
        g = lax.dot_general(d.reshape(3, head_cols, rows), n, (((2,), (0,)), ((), ())), preferred_element_type=F32)
        return g.transpose(0, 2, 1).reshape(3 * width, head_cols).astype(BF16), jnp.sum(d, axis=1, dtype=F32)

    grad4, b_qkv_part = run(qkv_grad, d_qkv, normed)
    qkv = exchange(line, grad4, "dp")
    qkv.step()
    up1.step()

    def finish_down(*parts):
        n = len(parts) // 2
        return (jnp.concatenate([down0.whole(*parts[:n]), down1.whole(*parts[n:])], axis=1),)

    (w_down_grad,) = run(finish_down, *down0.parts(), *down1.parts())
    up1.step()
    qkv.step()
    (w_out_grad,) = run(lambda *p: (out.whole(*p),), *out.parts())
    up1.step()
    qkv.step()
    b_parts = small_sum(jnp.concatenate([b_up_part.value, b_qkv_part.value]), "dp")
    qkv.step()
    (result,) = run(lambda b: ((own + b.astype(F32) + out_bias).astype(BF16),), branch)

    def finish_up(*parts):
        n = len(parts) // 2
        return (jnp.concatenate([up0.whole(*parts[:n]), up1.whole(*parts[n:])], axis=0),)

    (w_up_grad,) = run(finish_up, *up0.parts(), *up1.parts())

    def norm_back(d, c):
        d = d.astype(F32)
        e = d * ln_gain
        pulled = c.astype(F32)
        grad = pulled + rsig * (
            e - jnp.mean(e, axis=-1, keepdims=True) - xhat * jnp.mean(e * xhat, axis=-1, keepdims=True)
        )
        sums = jnp.stack([jnp.sum(d * xhat, axis=0), jnp.sum(d, axis=0), jnp.sum(pulled, axis=0)])
        return grad, sums

    token_grad, sums = run(norm_back, d_normed, cot)
    sums = small_sum(small_sum(sums.value, axis), "dp")
    (w_qkv_grad,) = run(lambda *p: (qkv.whole(*p),), *qkv.parts())
    return (
        result.value,
        token_grad.value,
        sums[0],
        sums[1],
        w_qkv_grad.value.reshape(3, width, head_cols).transpose(1, 0, 2),
        b_parts[units:].reshape(3, head_cols),
        w_out_grad.value,
        w_up_grad.value,
        b_parts[:units],
        w_down_grad.value,
        sums[2],
    )


def solution(mesh):
    placed = (
        P(("dp", "tensor"), None),
        P(("dp", "tensor"), None),
        P(),
        P(),
        P(None, None, "tensor"),
        P(None, "tensor"),
        P("tensor", None),
        P(None, "tensor"),
        P("tensor"),
        P("tensor", None),
        P(),
    )
    return jax.shard_map(
        per_device, mesh=mesh, in_specs=placed, out_specs=placed, check_vma=False
    )
```
